32 devices in a mesh: groups: 2 (over y), tile: 4 (over z), line: 2 (over x), sub: 2 (over core).
Axes of the slice: x: 2, y: 2, z: 4, core: 2. Of those that a mesh axis runs over, the one named last changes fastest.
Arguments:
- traces: bfloat16 [4, 64, 1024, 1024], P(('groups', 'line'), None, 'tile', 'sub'), parts along dimension 0, may hold values from -6 to 6
- mute_index: int32 [1024], replicated, may hold values from 0 to 15
- freq_bins: int32 [4], replicated, may hold values from 0 to 3, each once
Outputs:
- multiples: float32 [2, 4, 2048, 1024], P(None, 'tile', ('groups', 'line'), 'sub'), parts along dimension 2
The draws below stay inside these ranges and needn't reach their ends.
There are 2 independent parts, one for each index of `groups`. The reference program is written for one: setup_inputs(seed, part) draws one part's arguments, and reference() takes and returns one part's arrays. A program takes and returns all parts, laid end to end along the dimension named above; an argument that names none is the same for every part. Nothing has to cross between parts.
Inputs may be any that keep to these rules, and one draw needn't show every extreme that they name: `freq_bins`: every bin number appears in exactly one slot.
All inputs are finite; a program needn't handle non-finite values.
Results may differ from the reference program's by a relative error of at most 0.0063.
Values may be sent and summed in bfloat16 or wider, within the bound.
No kernel may reach another device: no remote copies, remote signals or barrier semaphores. Data moves between devices by JAX's collectives and lax.ppermute only.
A program may use at most 64 MiB of HBM per device.

```python
import math
import jax
import jax.numpy as jnp
from jax import lax

NS = 1024
T_SIZE = 64
MUTE = 16
RAMP = 8
LINES = 2
NF = 4


def with_ends(array, rng, smallest, top_value):
    longest = array.shape.index(max(array.shape))
    spots = []
    for shift in (0, 1):
        where = [jax.random.randint(jax.random.fold_in(rng, axis), (), 0, length) for axis, length in enumerate(array.shape)]
        where[longest] = (where[longest] + shift) % array.shape[longest]
        spots.append(tuple(where))
    return array.at[spots[0]].set(smallest).at[spots[1]].set(top_value)


def steps_of(stream_key, shape, pieces, smallest, largest):
    factor_of, own = 1.0, jax.random.fold_in(stream_key, 6)
    for axis_at, shards_of in pieces:
        draws = jnp.exp(jax.random.uniform(jax.random.fold_in(own, axis_at), (shards_of,), jnp.float32, smallest / len(pieces), largest / len(pieces)))
        factor_of = factor_of * jnp.repeat(draws, shape[axis_at] // shards_of).reshape([-1 if axis == axis_at else 1 for axis in range(len(shape))])
    return factor_of


def noise(stream_key, dims, width, reach, split=(), held_as=jnp.bfloat16):
    level = steps_of(stream_key, dims, split, -0.22, 0.18) if split else 1.0
    drawn = jax.random.normal(stream_key, dims, jnp.float32) * width * level
    return jnp.minimum(jnp.maximum(drawn, -reach), reach).astype(held_as)


def setup_inputs(seed: int = 0, part: int = 0) -> dict:
    key_of = jax.random.split(jax.random.key(seed), 4)
    part_splits = jax.random.split(jax.random.fold_in(key_of[3], part), 4)
    return {
        "traces": noise(part_splits[0], (LINES, T_SIZE, NS, NS), 1.0, 6.0, ((0, 2), (2, 4), (3, 2))),
        "mute_index": with_ends(jax.random.randint(key_of[1], (NS,), 0, MUTE), jax.random.fold_in(key_of[1], 1), 0, MUTE - 1).astype(jnp.int32),
        "freq_bins": jax.random.permutation(key_of[2], NF).astype(jnp.int32),
    }


def taper_weights(mute_index):
    src_ids = jnp.arange(NS, dtype=jnp.int32)
    offsets = jnp.abs(src_ids[:, None] - src_ids[None, :])
    onsets = mute_index[offsets]
    sample_ids = jnp.arange(T_SIZE, dtype=jnp.int32)[:, None, None]
    ramp_pos = jnp.clip((sample_ids - onsets[None] + 1).astype(jnp.float32) / jnp.float32(RAMP + 1), 0.0, 1.0)
    return 0.5 - 0.5 * jnp.cos(jnp.float32(math.pi) * ramp_pos)

def build_table(freq_bins, samples):
    sample_ids = jnp.arange(samples, dtype=jnp.int32)
    phase = (freq_bins[:, None] * sample_ids[None, :] % samples).astype(jnp.float32) * jnp.float32(2.0 * math.pi / samples)
    factor = jnp.float32(1.0 / math.sqrt(samples))
    return jnp.concatenate([jnp.cos(phase) * factor, -jnp.sin(phase) * factor], axis=0).astype(jnp.bfloat16)

def reference(traces, mute_index, freq_bins):
    weights = taper_weights(mute_index)
    dft_table = build_table(freq_bins, T_SIZE)
    factor = jnp.float32(1.0 / math.sqrt(NS))
    high = lax.Precision.HIGHEST

    def one_line(running, line_traces):
        tapered = (line_traces.astype(jnp.float32) * weights).astype(jnp.bfloat16)
        spectra = jnp.dot(dft_table, tapered.reshape(T_SIZE, NS * NS), preferred_element_type=jnp.float32)
        spectra = spectra.astype(jnp.bfloat16).reshape(2, NF, NS, NS).astype(jnp.float32)
        symmetric = ((spectra + jnp.swapaxes(spectra, 2, 3)) * 0.5).astype(jnp.bfloat16).astype(jnp.float32)
        real_part = symmetric[0]
        imag_part = symmetric[1]
        prod_real = jnp.einsum('kab,kbc->kac', real_part, real_part, precision=high) - jnp.einsum('kab,kbc->kac', imag_part, imag_part, precision=high)
        prod_imag = jnp.einsum('kab,kbc->kac', real_part, imag_part, precision=high) + jnp.einsum('kab,kbc->kac', imag_part, real_part, precision=high)
        return (running + jnp.stack([prod_real, prod_imag]) * factor, None)
    start_sum = jnp.zeros((2, NF, NS, NS), jnp.float32)
    multiples, unused = lax.scan(one_line, start_sum, traces)
    return multiples
```

```python
import functools
import math

import jax
import jax.numpy as jnp
from jax import lax
from jax.experimental import pallas as pl
from jax.experimental.pallas import tpu as pltpu
from jax.sharding import PartitionSpec as P

RAMP = 8
LATEST = 15
LANES = 128
GROUP = 16
VMEM_BYTES = 56 * 2**20


def wave_tables(samples):
    phase = jnp.arange(LANES, dtype=jnp.int32) % samples
    phase = phase.astype(jnp.float32) * jnp.float32(2.0 * math.pi / samples)
    factor = jnp.float32(1.0 / math.sqrt(samples))
    return jnp.stack([jnp.cos(phase) * factor, -jnp.sin(phase) * factor])


def ramp_table():
    pos = jnp.clip(jnp.arange(LANES, dtype=jnp.float32) / jnp.float32(RAMP + 1), 0.0, 1.0)
    return (0.5 - 0.5 * jnp.cos(jnp.float32(math.pi) * pos))[None, :]


def ids(shape, axis):
    return lax.broadcasted_iota(jnp.int32, shape, axis)


def spread_table(bins_ref, place, waves_ref, samples, slots):
    rows = slots * 2 * GROUP
    wave = jnp.broadcast_to(waves_ref[0:1, :], (GROUP, LANES))
    other = jnp.broadcast_to(waves_ref[1:2, :], (GROUP, LANES))
    sample = ids((GROUP, LANES), 1)
    lines = []
    for d in range(slots):
        at = place + d
        at = jnp.where(at >= slots, at - slots, at)
        phase = (bins_ref[at] * sample) % samples
        lines.append(jnp.take_along_axis(wave, phase, axis=1))
        lines.append(jnp.take_along_axis(other, phase, axis=1))
    table = jnp.concatenate(lines, axis=0).astype(jnp.bfloat16)[:, :samples]
    wide = samples * GROUP
    pick = ids((samples, wide), 1) // GROUP == ids((samples, wide), 0)
    spread = jnp.dot(table, pick.astype(jnp.bfloat16), preferred_element_type=jnp.float32)
    keep = ids((rows, wide), 0) % GROUP == ids((rows, wide), 1) % GROUP
    return jnp.where(keep, spread, 0.0).astype(jnp.bfloat16)


def onset_window(start, mute_ref, wide):
    parts = mute_ref.shape[0]
    flip = ids((LANES, LANES), 0) + ids((LANES, LANES), 1) == LANES - 1
    mute = mute_ref[...].astype(jnp.float32)
    back = jnp.dot(
        mute.astype(jnp.bfloat16), flip.astype(jnp.bfloat16), preferred_element_type=jnp.float32
    )
    stations = parts * LANES
    tall = 8
    behind = [jnp.broadcast_to(back[i : i + 1, :], (tall, LANES)) for i in reversed(range(parts))]
    ahead = [jnp.broadcast_to(mute[i : i + 1, :], (tall, LANES)) for i in range(parts)]
    behind = pltpu.roll(jnp.concatenate(behind, axis=1), 1, 1)
    both = jnp.concatenate([behind] + ahead, axis=1)
    return pltpu.roll(both, 2 * stations - start, 1)[:, :wide].astype(jnp.int32)


def dft_kernel(
    tapered, base, rows, scalars_ref, bins_ref, x_ref, mute_ref, ramp_ref, waves_ref, *refs
):
    outs, (window_ref, onset_ref, table_ref) = refs[:-3], refs[-3:]
    samples = x_ref.shape[0]
    wide = window_ref.shape[1]
    step = pl.program_id(0)

    @pl.when(step == 0)
    def _():
        window_ref[...] = onset_window(scalars_ref[0], mute_ref, wide)
        table_ref[...] = spread_table(bins_ref, scalars_ref[1], waves_ref, samples, len(outs))

    window = jnp.broadcast_to(window_ref[0:1, :], (rows, wide))
    slanted = pltpu.roll(window, base, 1, stride=1, stride_axis=0)
    onset_ref[...] = pltpu.roll(slanted, step * rows, 1)[:, 0:LANES]
    ramp = jnp.broadcast_to(ramp_ref[0:1, :], (GROUP, LANES))
    for g in range(0, rows, 2 * GROUP):
        halves = []
        for s in (g, g + GROUP):
            onset = onset_ref[s : s + GROUP, :]
            parts = []
            for t in range(samples):
                x = x_ref[t, s : s + GROUP, :]
                if t < tapered:
                    at = jnp.clip(t + 1 - onset, 0, RAMP + 1)
                    weight = jnp.take_along_axis(ramp, at, axis=1)
                    x = (x.astype(jnp.float32) * weight).astype(jnp.bfloat16)
                parts.append(x)
            halves.append(jnp.concatenate(parts, axis=0))
        spectra = jnp.dot(
            table_ref[...], jnp.concatenate(halves, axis=1), preferred_element_type=jnp.float32
        ).astype(jnp.bfloat16)
        for d in range(len(outs)):
            for c in range(2):
                at = (d * 2 + c) * GROUP
                for i in range(2):
                    outs[d][c, g + i * GROUP : g + (i + 1) * GROUP, :] = spectra[
                        at : at + GROUP, i * LANES : (i + 1) * LANES
                    ]


def dft(scalars, bins, traces, mute, ramp, waves, chunk, slots, rows=64):
    samples, src_rows, rcv_cols = traces.shape
    rows = min(rows, src_rows)
    wide = -(-(src_rows + rcv_cols) // LANES) * LANES
    base = wide - src_rows - chunk * LANES
    tapered = min(samples, LATEST + RAMP)
    whole = lambda i, *_: (0, 0)
    return pl.pallas_call(
        functools.partial(dft_kernel, tapered, base, rows),
        grid_spec=pltpu.PrefetchScalarGridSpec(
            num_scalar_prefetch=2,
            grid=(src_rows // rows,),
            in_specs=[
                pl.BlockSpec((samples, rows, LANES), lambda i, *_: (0, i, chunk)),
                pl.BlockSpec(mute.shape, whole),
                pl.BlockSpec(ramp.shape, whole),
                pl.BlockSpec(waves.shape, whole),
            ],
            out_specs=[pl.BlockSpec((2, rows, LANES), lambda i, *_: (0, i, 0))] * slots,
            scratch_shapes=[
                pltpu.VMEM((8, wide), jnp.int32),
                pltpu.VMEM((rows, LANES), jnp.int32),
                pltpu.VMEM((slots * 2 * GROUP, samples * GROUP), jnp.bfloat16),
            ],
        ),
        out_shape=[jax.ShapeDtypeStruct((2, src_rows, LANES), jnp.bfloat16)] * slots,
        compiler_params=pltpu.CompilerParams(vmem_limit_bytes=32 * 2**20),
        cost_estimate=pl.CostEstimate(
            flops=2 * slots * 2 * samples * src_rows * LANES * GROUP,
            bytes_accessed=samples * src_rows * LANES * 2,
            transcendentals=0,
        ),
    )(scalars, bins, traces, mute, ramp, waves)


def collect_kernel(place_ref, *refs):
    blocks, out_ref = refs[:-1], refs[-1]
    slots = len(blocks)
    rows = blocks[0].shape[1]
    for d, block in enumerate(blocks):
        owner = place_ref[0] - d
        owner = jnp.where(owner < 0, owner + slots, owner)
        out_ref[:, pl.ds(pl.multiple_of(owner * rows, rows), rows), :] = block[...]


def collect(place, blocks):
    comps, rows, cols = blocks[0].shape
    vmem = pl.BlockSpec(memory_space=pltpu.VMEM)
    size = len(blocks) * comps * rows * cols
    return pl.pallas_call(
        collect_kernel,
        in_specs=[pl.BlockSpec(memory_space=pltpu.SMEM)] + [vmem] * len(blocks),
        out_specs=vmem,
        out_shape=jax.ShapeDtypeStruct((comps, len(blocks) * rows, cols), jnp.bfloat16),
        compiler_params=pltpu.CompilerParams(vmem_limit_bytes=16 * 2**20),
        cost_estimate=pl.CostEstimate(flops=size, bytes_accessed=4 * size, transcendentals=0),
    )(place, *blocks)


def square_kernel(lines, half, part, scalars_ref, *refs):
    blocks, (out_ref, sym_ref) = refs[:-2], refs[-2:]
    per_line = len(blocks) // lines
    stations = blocks[0].shape[1]
    first, row_at = scalars_ref[0], scalars_ref[1]
    here = first * half
    there = half - here

    def start(a):
        inner = a * LANES
        at = here + inner if inner < half else there + inner - half
        return pl.multiple_of(at, LANES)

    for line in range(lines):
        cols = blocks[line * per_line : (line + 1) * per_line]

        @pl.loop(0, 2)
        def _(c):
            for a in range(per_line):
                for b in range(a, per_line):
                    upper = cols[b][c, pl.ds(start(a), LANES), :].astype(jnp.float32)
                    lower = cols[a][c, pl.ds(start(b), LANES), :].astype(jnp.float32)
                    mean = (upper + lower.T) * 0.5
                    i, j = slice(a * LANES, (a + 1) * LANES), slice(b * LANES, (b + 1) * LANES)
                    sym_ref[c, i, j] = mean.astype(jnp.bfloat16)
                    if a != b:
                        sym_ref[c, j, i] = mean.T.astype(jnp.bfloat16)

        rows = pl.ds(pl.multiple_of(row_at, part), part)
        real_left, imag_left = sym_ref[0, rows, :], sym_ref[1, rows, :]
        real_right, imag_right = sym_ref[0, :, 0:half], sym_ref[1, :, 0:half]
        dot = functools.partial(jnp.dot, preferred_element_type=jnp.float32)
        real = dot(real_left, real_right) - dot(imag_left, imag_right)
        imag = dot(real_left, imag_right) + dot(imag_left, real_right)
        factor = jnp.float32(1.0 / math.sqrt(stations))
        if line == 0:
            out_ref[0, 0], out_ref[1, 0] = real * factor, imag * factor
        else:
            out_ref[0, 0] += real * factor
            out_ref[1, 0] += imag * factor


def square(scalars, blocks, lines, half):
    comps, stations, _ = blocks[0].shape
    part = stations // lines
    vmem = pl.BlockSpec(memory_space=pltpu.VMEM)
    return pl.pallas_call(
        functools.partial(square_kernel, lines, half, part),
        in_specs=[pl.BlockSpec(memory_space=pltpu.SMEM)] + [vmem] * len(blocks),
        out_specs=vmem,
        out_shape=jax.ShapeDtypeStruct((comps, 1, part, half), jnp.float32),
        scratch_shapes=[pltpu.VMEM((comps, stations, stations), jnp.bfloat16)],
        compiler_params=pltpu.CompilerParams(vmem_limit_bytes=VMEM_BYTES),
        cost_estimate=pl.CostEstimate(
            flops=8 * lines * part * half * stations,
            bytes_accessed=4 * lines * stations * stations,
            transcendentals=0,
        ),
    )(scalars, *blocks)


def shift(array, axis, step):
    count = lax.axis_size(axis)
    return lax.ppermute(array, axis, [(i, (i + step) % count) for i in range(count)])


def local(traces, mute_index, freq_bins):
    samples, src_rows, rcv_cols = traces.shape[1:]
    stations = mute_index.shape[0]
    owners, lines = lax.axis_size("tile"), lax.axis_size("line")
    place, side = lax.axis_index("tile"), lax.axis_index("sub")
    mute = mute_index.reshape(stations // LANES, LANES)
    ramp, waves = ramp_table(), wave_tables(samples)
    start = side * rcv_cols - (place + 1) * src_rows + stations
    scalars = jnp.stack([start, place])
    where = place[None]
    chunks = rcv_cols // LANES
    spectra = [
        dft(scalars, freq_bins, traces[0], mute, ramp, waves, m, owners) for m in range(chunks)
    ]
    held = [[[None] * chunks for _ in range(2)] for _ in range(lines)]
    for m in range(chunks):
        arrived = [spectra[m][0]] + [shift(spectra[m][d], "tile", d) for d in range(1, owners)]
        own = collect(where, arrived)
        for e in range(lines):
            passed = shift(own, "line", e) if e else own
            held[e][0][m] = passed
            held[e][1][m] = shift(passed, "sub", 1)
    part = stations // lines
    row = lax.axis_index("line") * part
    row = jnp.where(row // rcv_cols == side, row % rcv_cols, rcv_cols + row % rcv_cols)
    blocks = [block for line in held for owner in line for block in owner]
    return square(jnp.stack([side, row]), blocks, lines, rcv_cols)


def solution(mesh):
    return jax.shard_map(
        local,
        mesh=mesh,
        in_specs=(P(("groups", "line"), None, "tile", "sub"), P(), P()),
        out_specs=P(None, "tile", ("groups", "line"), "sub"),
        check_vma=False,
    )
```

```python
import functools
import math

import jax
import jax.numpy as jnp
from jax import lax
from jax.experimental import pallas as pl
from jax.experimental.pallas import tpu as pltpu
from jax.sharding import PartitionSpec as P


RAMP = 8
LATEST = 15
LANES = 128
GROUP = 16


def ids(shape, axis):
    return lax.broadcasted_iota(jnp.int32, shape, axis)


def ramp_table():
    pos = (ids((GROUP, LANES), 1) - GROUP).astype(jnp.float32)
    pos = jnp.clip(pos / jnp.float32(RAMP + 1), 0.0, 1.0)
    return 0.5 - 0.5 * jnp.cos(jnp.float32(math.pi) * pos)


def receiver(place, distance, count):
    if count & (count - 1) == 0:
        return place ^ distance, place ^ distance
    return (place + distance) % count, (place - distance) % count


def spread_table(bins_ref, place, samples, slots):
    rows = slots * 2 * GROUP
    bins = jnp.zeros((rows, LANES), jnp.int32)
    row = ids((rows, LANES), 0) // GROUP
    for k in range(slots):
        bins = jnp.where(row // 2 == k, bins_ref[receiver(place, k, slots)[0]], bins)
    phase = (bins * ids((rows, LANES), 1)) % samples
    angle = phase.astype(jnp.float32) * jnp.float32(2.0 * math.pi / samples)
    factor = jnp.float32(1.0 / math.sqrt(samples))
    table = jnp.where(row % 2 == 0, jnp.cos(angle) * factor, -jnp.sin(angle) * factor)
    table = table.astype(jnp.bfloat16)[:, :samples]
    wide = samples * GROUP
    pick = ids((samples, wide), 1) // GROUP == ids((samples, wide), 0)
    spread = jnp.dot(table, pick.astype(jnp.bfloat16), preferred_element_type=jnp.float32)
    keep = ids((rows, wide), 0) % GROUP == ids((rows, wide), 1) % GROUP
    return jnp.where(keep, spread, 0.0).astype(jnp.bfloat16)


def onset_window(start, mute_ref, wide):
    parts = mute_ref.shape[0]
    flip = ids((LANES, LANES), 0) + ids((LANES, LANES), 1) == LANES - 1
    mute = mute_ref[...].astype(jnp.float32)
    back = jnp.dot(
        mute.astype(jnp.bfloat16), flip.astype(jnp.bfloat16), preferred_element_type=jnp.float32
    )
    stations = parts * LANES
    tall = 8
    behind = [jnp.broadcast_to(back[i : i + 1, :], (tall, LANES)) for i in reversed(range(parts))]
    ahead = [jnp.broadcast_to(mute[i : i + 1, :], (tall, LANES)) for i in range(parts)]
    behind = pltpu.roll(jnp.concatenate(behind, axis=1), 1, 1)
    both = jnp.concatenate([behind] + ahead, axis=1)
    return pltpu.roll(both, 2 * stations - start, 1)[:, :wide].astype(jnp.int32)


def dft_kernel(tapered, base, src_rows, rows, slots, counts, bins_ref, x_ref, mute_ref, *refs):
    outs, (window_ref, index_ref, ramp_ref, table_ref) = refs[:-4], refs[-4:]
    own_ref, outs = outs[0], outs[1:]
    samples, _, width = x_ref.shape
    wide = window_ref.shape[1]
    step = pl.program_id(0)

    @pl.when(step == 0)
    def _():
        stations = mute_ref.shape[0] * LANES
        place, side = lax.axis_index("tile"), lax.axis_index("sub")
        start = side * width - (place + 1) * src_rows + stations
        window_ref[...] = onset_window(start, mute_ref, wide)
        ramp_ref[...] = ramp_table()
        table_ref[...] = spread_table(bins_ref, place, samples, slots)

    window = jnp.broadcast_to(window_ref[0:1, :], (rows, wide))
    slanted = pltpu.roll(window, base, 1, stride=1, stride_axis=0)
    index_ref[...] = GROUP + 1 - pltpu.roll(slanted, step * rows, 1)[:, 0:width]
    ramp = ramp_ref[...]
    for s in range(0, rows, GROUP):
        columns = []
        for r in range(0, width, LANES):
            at = index_ref[s : s + GROUP, r : r + LANES]
            parts = []
            for t in range(samples):
                x = x_ref[t, s : s + GROUP, r : r + LANES]
                if t < tapered:
                    weight = jnp.take_along_axis(ramp, at + t, axis=1)
                    x = (x.astype(jnp.float32) * weight).astype(jnp.bfloat16)
                parts.append(x)
            columns.append(jnp.concatenate(parts, axis=0))
        spectra = jnp.dot(
            table_ref[...], jnp.concatenate(columns, axis=1), preferred_element_type=jnp.float32
        ).astype(jnp.bfloat16)

        def put(out_ref, d):
            for c in range(2):
                at = (d * 2 + c) * GROUP
                out_ref[c, s : s + GROUP, :] = spectra[at : at + GROUP, :]

        put(own_ref, 0)
        begin = 0
        for m, count in enumerate(counts):

            @pl.when((step >= begin) & (step < begin + count // rows))
            def _():
                for d in range(1, slots):
                    put(outs[m * (slots - 1) + d - 1], d)

            begin += count // rows


def dft(bins, traces, mute, first, counts, slots):
    samples, src_rows, width = traces.shape
    total = sum(counts)
    rows = 2 * GROUP
    while any(n % rows for n in [first] + counts):
        rows //= 2
    wide = -(-(src_rows + width) // LANES) * LANES
    tapered = min(samples, LATEST + RAMP)

    def piece(begin, count):
        last = count // rows - 1
        return pl.BlockSpec(
            (2, rows, width), lambda i, *_: (0, jnp.clip(i - begin // rows, 0, last), 0)
        )

    outs, specs = [(2, total, width)], [piece(0, total)]
    for m, count in enumerate(counts):
        outs += [(2, count, width)] * (slots - 1)
        specs += [piece(sum(counts[:m]), count)] * (slots - 1)
    return pl.pallas_call(
        functools.partial(
            dft_kernel, tapered, wide - src_rows + first, src_rows, rows, slots, counts
        ),
        grid_spec=pltpu.PrefetchScalarGridSpec(
            num_scalar_prefetch=1,
            grid=(total // rows,),
            in_specs=[
                pl.BlockSpec((samples, rows, width), lambda i, *_: (0, i + first // rows, 0)),
                pl.BlockSpec(mute.shape, lambda i, *_: (0, 0)),
            ],
            out_specs=specs,
            scratch_shapes=[
                pltpu.VMEM((8, wide), jnp.int32),
                pltpu.VMEM((rows, width), jnp.int32),
                pltpu.VMEM((GROUP, LANES), jnp.float32),
                pltpu.VMEM((slots * 2 * GROUP, samples * GROUP), jnp.bfloat16),
            ],
        ),
        out_shape=[jax.ShapeDtypeStruct(shape, jnp.bfloat16) for shape in outs],
        compiler_params=pltpu.CompilerParams(
            vmem_limit_bytes=67_043_328
        ),
        cost_estimate=pl.CostEstimate(
            flops=4 * slots * samples * total * width * GROUP,
            bytes_accessed=samples * total * width * 2,
            transcendentals=0,
        ),
    )(bins, traces, mute)


def stack_kernel(at, count, slots, packed, own_ref, *refs):
    place = lax.axis_index("tile")
    blocks, outs = (refs[:1], refs[1:]) if packed else (refs[: slots - 1], refs[slots - 1 :])
    outs[0][place] = own_ref[:, at : at + count, :]
    for d in range(1, slots):
        block = blocks[0][d - 1] if packed else blocks[d - 1][...]
        outs[0][receiver(place, d, slots)[1]] = block
        if not packed:
            outs[1][d - 1] = block


def stack(own, at, blocks, slots):
    packed = len(blocks) == 1 and slots > 2
    comps, count, cols = blocks[0].shape[-3:]
    sizes = [slots] if packed else [slots, slots - 1]
    vmem = pl.BlockSpec(memory_space=pltpu.VMEM)
    size = slots * count * comps * cols
    return pl.pallas_call(
        functools.partial(stack_kernel, at, count, slots, packed),
        in_specs=[vmem] * (1 + len(blocks)),
        out_specs=[vmem] * len(sizes),
        out_shape=[jax.ShapeDtypeStruct((n, comps, count, cols), jnp.bfloat16) for n in sizes],
        compiler_params=pltpu.CompilerParams(vmem_limit_bytes=16 * 2**20),
        cost_estimate=pl.CostEstimate(flops=size, bytes_accessed=4 * size, transcendentals=0),
    )(own, *blocks)


def square_kernel(lines, half, part, counts, *refs):
    chunks = len(counts)
    per_line = 2 * chunks
    arrays = refs[: lines * per_line]
    out_ref, sym_ref = refs[lines * per_line :]
    src_rows = sum(counts)
    stations = 2 * half
    blocks = stations // LANES
    side = lax.axis_index("sub")
    row_at = lax.axis_index("line") * part
    row_at = jnp.where(row_at // half == side, 0, half) + row_at % half
    firsts = [sum(counts[:m]) for m in range(chunks)]

    def rows_of(sources, c, a, lanes):
        inner = a * LANES % half
        tile = (side if a * LANES < half else 1 - side) * (half // src_rows) + inner // src_rows
        pieces = []
        left, row = LANES, inner % src_rows
        while left:
            take = min(left, src_rows - row)
            for first, count, source in zip(firsts, counts, sources):
                lo, hi = max(row, first), min(row + take, first + count)
                if lo < hi:
                    pieces.append(source[tile, c, lo - first : hi - first, lanes])
            left, tile, row = left - take, tile + 1, 0
        return pieces[0] if len(pieces) == 1 else jnp.concatenate(pieces, axis=0)

    for line in range(lines):
        own = range(line * per_line, (line + 1) * per_line)
        sides = [[arrays[i] for i in own[s * chunks : (s + 1) * chunks]] for s in range(2)]

        def block(c, a, b):
            at = b * LANES % half
            lanes = slice(at, at + LANES)
            return rows_of(sides[b * LANES // half], c, a, lanes).astype(jnp.float32)

        @pl.loop(0, 2)
        def _(c):
            for a in range(blocks):
                for b in range(a, blocks):
                    mean = (block(c, a, b) + block(c, b, a).T) * 0.5
                    i, j = slice(a * LANES, (a + 1) * LANES), slice(b * LANES, (b + 1) * LANES)
                    sym_ref[c, i, j] = mean.astype(jnp.bfloat16)
                    if a != b:
                        sym_ref[c, j, i] = mean.T.astype(jnp.bfloat16)

        rows = pl.ds(pl.multiple_of(row_at, part), part)
        real_left, imag_left = sym_ref[0, rows, :], sym_ref[1, rows, :]
        real_right, imag_right = sym_ref[0, :, 0:half], sym_ref[1, :, 0:half]
        dot = functools.partial(jnp.dot, preferred_element_type=jnp.float32)
        real = dot(real_left, real_right) - dot(imag_left, imag_right)
        imag = dot(real_left, imag_right) + dot(imag_left, real_right)
        factor = jnp.float32(1.0 / math.sqrt(stations))
        if line == 0:
            out_ref[0, 0], out_ref[1, 0] = real * factor, imag * factor
        else:
            out_ref[0, 0] += real * factor
            out_ref[1, 0] += imag * factor


def square(held, lines, half, counts):
    stations = 2 * half
    part = stations // lines
    return pl.pallas_call(
        functools.partial(square_kernel, lines, half, part, counts),
        in_specs=[pl.BlockSpec(memory_space=pltpu.VMEM)] * len(held),
        out_specs=pl.BlockSpec(memory_space=pltpu.VMEM),
        out_shape=jax.ShapeDtypeStruct((2, 1, part, half), jnp.float32),
        scratch_shapes=[pltpu.VMEM((2, stations, stations), jnp.bfloat16)],
        compiler_params=pltpu.CompilerParams(vmem_limit_bytes=36 * 2**20),
        cost_estimate=pl.CostEstimate(
            flops=8 * lines * part * half * stations,
            bytes_accessed=4 * lines * stations * stations,
            transcendentals=0,
        ),
    )(*held)


def shift(array, axis, step):
    count = lax.axis_size(axis)
    return lax.ppermute(array, axis, [(i, (i + step) % count) for i in range(count)])


def row_chunks(src_rows):
    units = src_rows // GROUP
    if units < 8:
        return [[src_rows]]
    last, some = units // 8, units // 4
    return [[(units - last - 2 * some) * GROUP], [some * GROUP, some * GROUP, last * GROUP]]


def send(array, distance):
    count = lax.axis_size("tile")
    pairs = [(i, receiver(i, distance, count)[0]) for i in range(count)]
    return lax.ppermute(array, "tile", pairs)


def local(traces, mute_index, freq_bins):
    src_rows, rcv_cols = traces.shape[2:]
    owners, lines = lax.axis_size("tile"), lax.axis_size("line")
    mute = mute_index.reshape(-1, LANES)
    groups = row_chunks(src_rows)
    counts = [count for group in groups for count in group]
    chunks = len(counts)
    held = [[[None] * chunks for _ in range(2)] for _ in range(lines)]
    first, made = 0, []
    for group in groups:
        own, *blocks = dft(freq_bins, traces[0], mute, first, group, owners)
        first += sum(group)
        at = 0
        passed = [shift(own, "line", e) for e in range(1, lines)]
        for m, count in enumerate(group):
            pieces = blocks[m * (owners - 1) : (m + 1) * (owners - 1)]
            arrived = [None] * (owners - 1)
            for d in reversed(range(1, owners)):
                arrived[d - 1] = send(pieces[d - 1], d)
            made.append((own, passed, at, arrived))
            at += count
    for m, (own, passed, at, arrived) in enumerate(made):
        whole, rest = stack(own, at, arrived, owners)
        held[0][0][m], held[0][1][m] = whole, shift(whole, "sub", 1)
        for e in range(1, lines):
            rest_e = shift(rest, "line", e)
            (other,) = stack(passed[e - 1], at, [rest_e], owners)
            held[e][0][m], held[e][1][m] = other, shift(other, "sub", 1)
    arrays = [array for line in held for side in line for array in side]
    return square(arrays, lines, rcv_cols, counts)


def solution(mesh):
    return jax.shard_map(
        local,
        mesh=mesh,
        in_specs=(P(("groups", "line"), None, "tile", "sub"), P(), P()),
        out_specs=P(None, "tile", ("groups", "line"), "sub"),
        check_vma=False,
    )
```
